128 devices in a mesh: dp: 8 (over z, core), seq: 16 (over y, x).
Axes of the slice: x: 4, y: 4, z: 4, core: 2. Of those that a mesh axis runs over, the one named last changes fastest.
Arguments:
- queries: bfloat16 [8, 2048, 2048], P('dp', 'seq'), may hold values from -34 to 34
- key_rows: bfloat16 [8, 2048, 2048], P('dp', 'seq'), may hold values from -34 to 34
- values: bfloat16 [8, 2048, 2048], P('dp', 'seq'), may hold values from -6 to 6
- adjacency: int32 [8, 16, 8], P('dp'), may hold values from 0 to 15, as said below
- counts: int32 [8, 16], P('dp'), may hold values from 1 to 8, as said below
- out_weight: bfloat16 [2048, 2048], P('dp'), may hold values from -0.125 to 0.125
- out_cotangent: bfloat16 [8, 2048, 2048], P('dp', 'seq'), may hold values from -6 to 6
Outputs:
- layer_out: bfloat16 [8, 2048, 2048], P('dp', 'seq')
- query_grad: bfloat16 [8, 2048, 2048], P('dp', 'seq')
- key_grad: bfloat16 [8, 2048, 2048], P('dp', 'seq')
- value_grad: bfloat16 [8, 2048, 2048], P('dp', 'seq')
- weight_grad: float32 [2048, 2048], P(('dp', 'seq'))
The draws below stay inside these ranges and needn't reach their ends.
Inputs may be any that keep to these rules, and one draw needn't show every extreme that they name: `adjacency`: row i of a sequence lists 8 different key blocks, slot 0 being block i itself; slots at or beyond the row's count are not attended. `counts`: block 0 of every sequence has all 8 slots live.
All inputs are finite; a program needn't handle non-finite values.
Results may differ from the reference program's by a relative error of at most 0.025.
Values may be sent and summed in bfloat16 or wider, within the bound.
A program may use at most 128 MiB of HBM per device.

```python
import jax
import jax.numpy as jnp
from jax import lax

D = 2048
H = 16
HD = 128
BLK = 128
NBR = 8
SEQS = 8
LEN = 2048
NBLK = 16


def paired(key):
    base = jax.random.fold_in(key, 11)
    first, second = jax.random.split(base, 2)
    shape = (SEQS, LEN, D)
    query_draw = 1.6 * jnp.clip(jax.random.normal(first, shape, jnp.float32), -6.0, 6.0)
    key_draw = 1.6 * jnp.clip(jax.random.normal(second, shape, jnp.float32), -6.0, 6.0)
    return (query_draw, key_draw)


def graph(key):
    base = jax.random.fold_in(key, 29)
    count_key, order_key = jax.random.split(base)
    live = jax.random.randint(count_key, (SEQS, NBLK), 1, NBR + 1)
    live = live.at[:, 0].set(NBR)
    row_keys = jax.random.split(order_key, SEQS * NBLK)
    offsets = jax.vmap(lambda row_key: jax.random.permutation(row_key, NBLK - 1)[:NBR - 1])(row_keys)
    own_block = jnp.arange(SEQS * NBLK) % NBLK
    others = (own_block[:, None] + 1 + offsets) % NBLK
    links = jnp.concatenate([own_block[:, None], others], axis=1).reshape(SEQS, NBLK, NBR)
    return (links.astype(jnp.int32), live.astype(jnp.int32))


def draw_queries(key, part):
    return paired(key)[0].astype(jnp.bfloat16)


def draw_key_rows(key, part):
    return paired(key)[1].astype(jnp.bfloat16)


def draw_adjacency(key, part):
    return graph(key)[0]


def draw_counts(key, part):
    return graph(key)[1]


def block_scale(stream_key, dims, shards, least, top_value):
    level = 1.0
    for dim, shards_of in shards:
        draws = jax.random.uniform(jax.random.fold_in(jax.random.fold_in(stream_key, 6), dim), (shards_of,), jnp.float32, least / len(shards), top_value / len(shards))
        level = level * jnp.repeat(jnp.exp(draws), dims[dim] // shards_of).reshape((-1,) + (1,) * (len(dims) - 1 - dim))
    return level


def scatter_about(stream_key, dims, spread, limit, pieces=(), dtype=jnp.bfloat16):
    drawn = spread * jax.random.normal(stream_key, dims, jnp.float32)
    if pieces:
        drawn = drawn * block_scale(stream_key, dims, pieces, -0.22, 0.18)
    return jnp.clip(drawn, -limit, limit).astype(dtype)


def setup_inputs(seed: int = 0) -> dict:
    seeds = jax.random.split(jax.random.key(seed), 8)
    queries = draw_queries(jax.random.fold_in(seeds[7], 71), 0)
    key_rows = draw_key_rows(jax.random.fold_in(seeds[7], 71), 0)
    values = scatter_about(seeds[2], (SEQS, LEN, D), 1.0, 6.0, ((0, 8), (1, 16)))
    adjacency = draw_adjacency(jax.random.fold_in(seeds[7], 71), 0)
    counts = draw_counts(jax.random.fold_in(seeds[7], 71), 0)
    out_weight = scatter_about(seeds[5], (D, D), D ** -0.5, 0.125, ((0, 8),))
    out_cotangent = scatter_about(seeds[6], (SEQS, LEN, D), 1.0, 6.0, ((0, 8), (1, 16)))
    return {"queries": queries, "key_rows": key_rows, "values": values, "adjacency": adjacency, "counts": counts, "out_weight": out_weight, "out_cotangent": out_cotangent}


def attend(query_blk, key_blk, value_blk, links, live_count):
    scale = HD ** -0.5
    heads = query_blk.shape[2]
    key_near = key_blk[links].reshape(NBLK, NBR * BLK, heads, HD)
    value_near = value_blk[links].reshape(NBLK, NBR * BLK, heads, HD)
    scores = jnp.einsum("iqhd,ikhd->hiqk", query_blk.astype(jnp.float32), key_near.astype(jnp.float32)) * scale
    live = (jnp.arange(NBR * BLK) // BLK)[None, :] < live_count[:, None]
    scores = jnp.where(live[None, :, None, :], scores, -1e30)
    highest = jnp.max(scores, axis=-1, keepdims=True)
    expo = jnp.exp(scores - highest)
    prob = expo / jnp.sum(expo, axis=-1, keepdims=True)
    prob_bf = prob.astype(jnp.bfloat16)
    attended = jnp.einsum("hiqk,ikhd->iqhd", prob_bf.astype(jnp.float32), value_near.astype(jnp.float32)).astype(jnp.bfloat16)
    return prob, prob_bf, attended, key_near, value_near


def backward(query_blk, key_blk, value_blk, links, live_count, grad_blk):
    scale = HD ** -0.5
    heads = query_blk.shape[2]
    prob, prob_bf, attended, key_near, value_near = attend(query_blk, key_blk, value_blk, links, live_count)
    grad_f = grad_blk.astype(jnp.float32)
    value_part = jnp.einsum("hiqk,iqhd->ikhd", prob_bf.astype(jnp.float32), grad_f)
    grad_prob = jnp.einsum("iqhd,ikhd->hiqk", grad_f, value_near.astype(jnp.float32))
    delta = jnp.einsum("iqhd,iqhd->hiq", grad_f, attended.astype(jnp.float32))
    score_grad = (prob * (grad_prob - delta[..., None]) * scale).astype(jnp.bfloat16)
    query_grad = jnp.einsum("hiqk,ikhd->iqhd", score_grad.astype(jnp.float32), key_near.astype(jnp.float32)).astype(jnp.bfloat16)
    key_part = jnp.einsum("hiqk,iqhd->ikhd", score_grad.astype(jnp.float32), query_blk.astype(jnp.float32))
    flat = links.reshape(-1)
    empty = jnp.zeros((NBLK, BLK, heads, HD), jnp.float32)
    key_grad = empty.at[flat].add(key_part.reshape(NBLK * NBR, BLK, heads, HD)).astype(jnp.bfloat16)
    value_grad = empty.at[flat].add(value_part.reshape(NBLK * NBR, BLK, heads, HD)).astype(jnp.bfloat16)
    return query_grad, key_grad, value_grad


def blocks_of(tokens):
    return tokens.reshape(NBLK, BLK, H, HD)


def reference(queries, key_rows, values, adjacency, counts, out_weight, out_cotangent):
    def forward_one(items):
        query_tok, key_tok, value_tok, links, live_count = items
        attended = attend(blocks_of(query_tok), blocks_of(key_tok), blocks_of(value_tok), links, live_count)[2]
        return attended.reshape(LEN, D)

    attn = lax.map(forward_one, (queries, key_rows, values, adjacency, counts))
    flat_attn = attn.reshape(SEQS * LEN, D)
    flat_cot = out_cotangent.reshape(SEQS * LEN, D)
    layer_out = jnp.dot(flat_attn, out_weight, preferred_element_type=jnp.float32).astype(jnp.bfloat16).reshape(SEQS, LEN, D)
    grad_attn = lax.dot_general(flat_cot, out_weight, (((1,), (1,)), ((), ())), preferred_element_type=jnp.float32)
    grad_attn = grad_attn.astype(jnp.bfloat16).reshape(SEQS, LEN, D)
    weight_grad = lax.dot_general(flat_attn, flat_cot, (((0,), (0,)), ((), ())), preferred_element_type=jnp.float32)

    def backward_one(items):
        query_tok, key_tok, value_tok, links, live_count, grad_tok = items
        grads = backward(blocks_of(query_tok), blocks_of(key_tok), blocks_of(value_tok), links, live_count, blocks_of(grad_tok))
        return tuple(part.reshape(LEN, D) for part in grads)

    query_grad, key_grad, value_grad = lax.map(backward_one, (queries, key_rows, values, adjacency, counts, grad_attn))
    return layer_out, query_grad, key_grad, value_grad, weight_grad
```

```python
import functools

import jax
import jax.numpy as jnp
from jax import lax
from jax.experimental import pallas as pl
from jax.experimental.pallas import tpu as pltpu
from jax.sharding import PartitionSpec as P

MESH = pl.DeviceIdType.MESH
HD = 128
BLK = 128
NBR = 8
NSEQ = 16
NDP = 8
NZ = 4
D = 2048
LEN = 2048
WROWS = D // NDP
SCALE = HD ** (-0.5)
F32 = jnp.float32
BF16 = jnp.bfloat16


def place():
    dp = lax.axis_index("dp")
    seq = lax.axis_index("seq")
    return dp, seq, dp // 2, dp % 2


def other_dp(z, c, dz, dc):
    return lax.rem(z + dz, NZ) * 2 + (lax.rem(c + dc, 2))


def remote(src, dst, send_sem, recv_sem, dp, seq):
    return pltpu.make_async_remote_copy(
        src_ref=src,
        dst_ref=dst,
        send_sem=send_sem,
        recv_sem=recv_sem,
        device_id=(dp, seq),
        device_id_type=MESH,
    )


def greet(partners):
    barrier = pltpu.get_barrier_semaphore()
    for dp, seq in partners:
        pl.semaphore_signal(barrier, inc=1, device_id=(dp, seq), device_id_type=MESH)
    pl.semaphore_wait(barrier, len(partners))


class DpGather:
    def __init__(self, own, slots, send_sem, recv_sem):
        self.dp, self.seq, self.z, self.c = place()
        self.own, self.slots, self.send_sem, self.recv_sem = own, slots, send_sem, recv_sem
        self.half = own.shape[0] // 2
        self.sends = []

    def dev(self, dz, dc):
        return other_dp(self.z, self.c, dz, dc)

    def send(self, src, dst, recv, dz, dc):
        copy = remote(
            src, dst, self.send_sem.at[len(self.sends)], self.recv_sem.at[recv], self.dev(dz, dc), self.seq
        )
        copy.start()
        self.sends.append(copy)

    def start(self):
        self.send(self.own, self.slots.at[6], 6, 1, 0)
        self.send(self.own, self.slots.at[2], 2, 3, 0)
        self.send(self.own, self.slots.at[1], 1, 0, 1)

    def await_slot(self, ref, recv):
        remote(ref, ref, self.send_sem.at[0], self.recv_sem.at[recv], self.dp, self.seq).wait_recv()

    def arrive(self, o):
        half = self.half
        if o == 4:
            self.await_slot(self.slots.at[4, pl.ds(0, half)], 4)
            self.await_slot(self.slots.at[4, pl.ds(half, half)], 8)
        else:
            self.await_slot(self.slots.at[o], o)
        if o == 2:
            self.send(self.slots.at[2, pl.ds(0, half)], self.slots.at[4, pl.ds(0, half)], 4, 3, 0)
        if o == 6:
            self.send(self.slots.at[6, pl.ds(half, half)], self.slots.at[4, pl.ds(half, half)], 8, 1, 0)
        if o in (2, 4, 6):
            self.send(self.slots.at[o], self.slots.at[o + 1], o + 1, 0, 1)

    def finish(self):
        for copy in self.sends:
            copy.wait_send()


GATHER_ORDER = (0, 1, 2, 6, 3, 7, 4, 5)


def spread_kernel(
    q_ref, k_ref, v_ref, cot_hbm, w_hbm,
    qh_ref, kh_ref, vh_ref, gh_ref, wfull_ref,
    cot, wbuf, gbuf,
    a2a_send, a2a_recv, g_send, g_recv, w_send, w_recv, loc_sem, own_sem, wout_sem,
):
    dp, seq, z, c = place()
    greet(
        [(dp, lax.rem(seq + r, NSEQ)) for r in range(1, NSEQ)]
        + [(other_dp(z, c, dz, dc), seq) for dz, dc in ((1, 0), (3, 0), (0, 1))]
    )
    load_cot = pltpu.make_async_copy(cot_hbm, cot, loc_sem.at[0])
    load_cot.start()
    load_w = pltpu.make_async_copy(w_hbm, wbuf.at[0], loc_sem.at[1])
    load_w.start()
    gather = DpGather(w_hbm, wbuf, w_send, w_recv)
    gather.start()
    here = pl.ds(pl.multiple_of(seq * BLK, BLK), BLK)
    pairs = ((q_ref, qh_ref), (k_ref, kh_ref), (v_ref, vh_ref))
    copies = []
    own_copies = []
    for n, (src, dst) in enumerate(pairs):
        for r in range(1, NSEQ):
            to = lax.rem(seq + r, NSEQ)
            copy = remote(
                src.at[:, pl.ds(pl.multiple_of(to * HD, HD), HD)],
                dst.at[here],
                a2a_send.at[n, r],
                a2a_recv.at[n, r],
                dp,
                to,
            )
            copy.start()
            copies.append(copy)
        copy = pltpu.make_async_copy(
            src.at[:, pl.ds(pl.multiple_of(seq * HD, HD), HD)], dst.at[here], own_sem.at[n]
        )
        copy.start()
        own_copies.append(copy)

    load_cot.wait()
    load_w.wait()
    wout = []

    def ship(o):
        owner = other_dp(z, c, o // 2, o % 2)
        for j in range(2):
            head = owner * 2 + j
            r = lax.rem(head - seq + NSEQ, NSEQ)
            src = gbuf.at[2 * o + j]

            @pl.when(r != 0)
            def _():
                remote(src, gh_ref.at[here], g_send.at[2 * o + j], g_recv.at[r], dp, head).start()

            @pl.when(r == 0)
            def _():
                pltpu.make_async_copy(src, gh_ref.at[here], g_send.at[2 * o + j]).start()

    last = None
    for o in GATHER_ORDER:
        if o:
            gather.arrive(o)
        owner = other_dp(z, c, o // 2, o % 2)
        copy = pltpu.make_async_copy(
            wbuf.at[o], wfull_ref.at[pl.ds(pl.multiple_of(owner * WROWS, WROWS), WROWS)], wout_sem.at[o]
        )
        copy.start()
        wout.append(copy)
        block = lax.dot_general(cot[...], wbuf[o], (((1,), (1,)), ((), ())), preferred_element_type=F32)
        for j in range(2):
            gbuf[2 * o + j] = block[:, j * HD : (j + 1) * HD].astype(BF16)
        if last is not None:
            ship(last)
        last = o
    ship(last)
    for copy in copies:
        copy.wait()
    for copy in own_copies + wout:
        copy.wait()
    gather.finish()
    for i in range(NSEQ):
        remote(gbuf.at[i], gbuf.at[i], g_send.at[i], g_recv.at[0], dp, seq).wait_send()
    for r in range(1, NSEQ):
        remote(gbuf.at[0], gh_ref.at[here], g_send.at[0], g_recv.at[r], dp, seq).wait_recv()


def spread(q, k, v, cot, w):
    head = jax.ShapeDtypeStruct((LEN, HD), BF16)
    any_spec = pl.BlockSpec(memory_space=pl.ANY)
    dma = pltpu.SemaphoreType.DMA
    return pl.pallas_call(
        spread_kernel,
        out_shape=(head, head, head, head, jax.ShapeDtypeStruct((D, D), BF16)),
        in_specs=[any_spec] * 5,
        out_specs=(any_spec,) * 5,
        scratch_shapes=[
            pltpu.VMEM((BLK, D), BF16),
            pltpu.VMEM((NDP, WROWS, D), BF16),
            pltpu.VMEM((NSEQ, BLK, HD), BF16),
            dma((3, NSEQ)),
            dma((3, NSEQ)),
            dma((NSEQ,)),
            dma((NSEQ,)),
            dma((8,)),
            dma((9,)),
            dma((2,)),
            dma((3,)),
            dma((NDP,)),
        ],
        compiler_params=pltpu.CompilerParams(collective_id=0, has_side_effects=True),
        name="spread",
    )(q, k, v, cot, w)


def attention_kernel(
    adj_ref, cnt_ref, q_ref, k_ref, v_ref, g_ref,
    o_ref, dq_ref, dk_ref, dv_ref,
    kt, vt, kg, vg, kgt, vgt, dk_acc, dv_acc,
):
    dk_acc[...] = jnp.zeros_like(dk_acc)
    dv_acc[...] = jnp.zeros_like(dv_acc)

    @pl.loop(0, LEN // BLK)
    def _(i):
        rows = pl.ds(pl.multiple_of(i * BLK, BLK), BLK)
        kt[i] = k_ref[rows, :].T
        vt[i] = v_ref[rows, :].T

    def run(i, slots):
        keys = slots * BLK
        rows = pl.ds(pl.multiple_of(i * BLK, BLK), BLK)
        q = q_ref[rows, :]
        g = g_ref[rows, :]
        count = cnt_ref[0, i]
        for j in range(slots):
            near = adj_ref[0, i, j]
            src = pl.ds(pl.multiple_of(near * BLK, BLK), BLK)
            dst = slice(j * BLK, (j + 1) * BLK)
            kg[dst, :] = k_ref[src, :]
            vg[dst, :] = v_ref[src, :]
            kgt[:, dst] = kt[near]
            vgt[:, dst] = vt[near]
        s = lax.dot_general(kg[:keys, :], q, (((1,), (1,)), ((), ())), preferred_element_type=F32) * SCALE
        live = lax.broadcasted_iota(jnp.int32, (keys, BLK), 0) < count * BLK
        s = jnp.where(live, s, -1e30)
        e = jnp.exp(s - jnp.max(s, axis=0, keepdims=True))
        p = e * (1.0 / jnp.sum(e, axis=0, keepdims=True))
        pb = p.astype(BF16)
        ot = jnp.dot(vgt[:, :keys], pb, preferred_element_type=F32)
        o_ref[rows, :] = ot.T.astype(BF16)
        dp = lax.dot_general(vg[:keys, :], g, (((1,), (1,)), ((), ())), preferred_element_type=F32)
        delta = jnp.sum(p * dp, axis=0, keepdims=True)
        ds = (p * (dp - delta) * SCALE).astype(BF16)
        dqt = jnp.dot(kgt[:, :keys], ds, preferred_element_type=F32)
        dq_ref[rows, :] = dqt.T.astype(BF16)
        dv = jnp.dot(pb, g, preferred_element_type=F32)
        dk = jnp.dot(ds, q, preferred_element_type=F32)
        for j in range(slots):
            near = adj_ref[0, i, j]
            dst = pl.ds(pl.multiple_of(near * BLK, BLK), BLK)
            part = slice(j * BLK, (j + 1) * BLK)
            dv_acc[dst, :] += dv[part, :]
            dk_acc[dst, :] += dk[part, :]

    @pl.loop(0, LEN // BLK)
    def _(i):
        count = cnt_ref[0, i]
        for slots in (2, 4, 6, 8):

            @pl.when((count > slots - 2) & (count <= slots))
            def _():
                run(i, slots)

    dk_ref[...] = dk_acc[...].astype(BF16)
    dv_ref[...] = dv_acc[...].astype(BF16)


def attention(adjacency, counts, q, k, v, g):
    head = jax.ShapeDtypeStruct((LEN, HD), BF16)
    vmem = pl.BlockSpec(memory_space=pltpu.VMEM)
    smem = pl.BlockSpec(memory_space=pltpu.SMEM)
    keys = NBR * BLK
    return pl.pallas_call(
        attention_kernel,
        out_shape=(head,) * 4,
        in_specs=[smem, smem] + [vmem] * 4,
        out_specs=(vmem,) * 4,
        scratch_shapes=[
            pltpu.VMEM((LEN // BLK, HD, BLK), BF16),
            pltpu.VMEM((LEN // BLK, HD, BLK), BF16),
            pltpu.VMEM((keys, HD), BF16),
            pltpu.VMEM((keys, HD), BF16),
            pltpu.VMEM((HD, keys), BF16),
            pltpu.VMEM((HD, keys), BF16),
            pltpu.VMEM((LEN, HD), F32),
            pltpu.VMEM((LEN, HD), F32),
        ],
        name="attention",
    )(adjacency, counts, q, k, v, g)


def collect_kernel(
    o_hbm, dq_hbm, dk_hbm, dv_hbm, w_hbm, cot_hbm,
    out_ref, dq_ref, dk_ref, dv_ref, wg_ref,
    w, cg, cols, near, near_t, part, terms, out_buf, wg_buf,
    o_send, o_recv, a2a_send, a2a_recv, c_send, c_recv, n_send, n_recv, t_send, t_recv, loc_sem,
):
    dp, seq, z, c = place()
    offsets = [(dz, dc) for dz in range(NZ) for dc in range(2) if dz or dc]
    greet(
        [(dp, lax.rem(seq + r, NSEQ)) for r in range(1, NSEQ)]
        + [(other_dp(z, c, dz, dc), seq) for dz, dc in offsets]
    )
    gather = DpGather(cot_hbm, cg, c_send, c_recv)
    gather.start()
    mine = pl.ds(pl.multiple_of(seq * HD, HD), HD)

    def exchange(src, dst, send_sem, recv_sem):
        copies = []
        for r in range(1, NSEQ):
            to = lax.rem(seq + r, NSEQ)
            copy = remote(
                src.at[pl.ds(pl.multiple_of(to * BLK, BLK), BLK)],
                dst.at[:, mine],
                send_sem.at[r],
                recv_sem.at[r],
                dp,
                to,
            )
            copy.start()
            copies.append(copy)
        return copies

    own_rows = pl.ds(pl.multiple_of(seq * BLK, BLK), BLK)
    attn_copies = exchange(o_hbm, cols, o_send, o_recv)
    own_attn = pltpu.make_async_copy(o_hbm.at[own_rows], cols.at[:, mine], loc_sem.at[0])
    own_attn.start()
    load_cot = pltpu.make_async_copy(cot_hbm, cg.at[0], loc_sem.at[1])
    load_cot.start()
    load_w = pltpu.make_async_copy(w_hbm, w, loc_sem.at[2])
    load_w.start()
    grad_copies = []
    own_copies = []
    for n, (src, dst) in enumerate(((dq_hbm, dq_ref), (dk_hbm, dk_ref), (dv_hbm, dv_ref))):
        grad_copies += exchange(src, dst, a2a_send.at[n], a2a_recv.at[n])
        copy = pltpu.make_async_copy(src.at[own_rows], dst.at[:, mine], loc_sem.at[3 + n])
        copy.start()
        own_copies.append(copy)

    own_attn.wait()
    for copy in attn_copies:
        copy.wait_recv()

    near_copies = []
    for n, (dz, dc) in enumerate(offsets):
        to = other_dp(z, c, dz, dc)
        o = ((NZ - dz) % NZ) * 2 + dc
        copy = remote(
            cols.at[:, pl.ds(pl.multiple_of(to * WROWS, WROWS), WROWS)],
            near.at[pl.ds(o * BLK, BLK)],
            n_send.at[n],
            n_recv.at[o],
            to,
            seq,
        )
        copy.start()
        near_copies.append(copy)
    near[pl.ds(0, BLK), :] = cols[:, pl.ds(pl.multiple_of(dp * WROWS, WROWS), WROWS)]

    load_w.wait()

    @pl.loop(0, D // 256)
    def _(n):
        at = pl.ds(pl.multiple_of(n * 256, 256), 256)
        out_buf[:, at] = jnp.dot(cols[...], w[:, at], preferred_element_type=F32).astype(BF16)

    store_out = pltpu.make_async_copy(out_buf, out_ref, loc_sem.at[6])
    store_out.start()

    load_cot.wait()
    for o in GATHER_ORDER[1:]:
        gather.arrive(o)
    for copy in near_copies:
        copy.wait_recv()
    near_t[...] = near[...].T

    @pl.loop(0, D // 256)
    def _(n):
        at = pl.ds(pl.multiple_of(n * 256, 256), 256)
        total = jnp.zeros((WROWS, 256), F32)
        for o in range(NDP):
            total += jnp.dot(near_t[:, o * BLK : (o + 1) * BLK], cg[o, :, at], preferred_element_type=F32)
        part[:, at] = total.astype(BF16)

    term_copies = []
    rows_out = D // (NDP * NSEQ)
    for r in range(1, NSEQ):
        to = lax.rem(seq + r, NSEQ)
        copy = remote(
            part.at[pl.ds(pl.multiple_of(to * rows_out, rows_out), rows_out)],
            terms.at[r],
            t_send.at[r],
            t_recv.at[r],
            dp,
            to,
        )
        copy.start()
        term_copies.append(copy)
    total = part[pl.ds(pl.multiple_of(seq * rows_out, rows_out), rows_out), :].astype(F32)
    for r in range(1, NSEQ):
        term_copies[r - 1].wait_recv()
        total += terms[r].astype(F32)
    wg_buf[...] = total
    store_wg = pltpu.make_async_copy(wg_buf, wg_ref, loc_sem.at[7])
    store_wg.start()

    for copy in grad_copies:
        copy.wait()
    for copy in attn_copies + near_copies + term_copies:
        copy.wait_send()
    for copy in own_copies:
        copy.wait()
    gather.finish()
    store_out.wait()
    store_wg.wait()


def collect(o, dq, dk, dv, w, cot):
    tokens = jax.ShapeDtypeStruct((BLK, D), BF16)
    any_spec = pl.BlockSpec(memory_space=pl.ANY)
    dma = pltpu.SemaphoreType.DMA
    rows_out = D // (NDP * NSEQ)
    return pl.pallas_call(
        collect_kernel,
        out_shape=(tokens,) * 4 + (jax.ShapeDtypeStruct((rows_out, D), F32),),
        in_specs=[any_spec] * 6,
        out_specs=(any_spec,) * 5,
        scratch_shapes=[
            pltpu.VMEM((D, D), BF16),
            pltpu.VMEM((NDP, BLK, D), BF16),
            pltpu.VMEM((BLK, D), BF16),
            pltpu.VMEM((NDP * BLK, WROWS), BF16),
            pltpu.VMEM((WROWS, NDP * BLK), BF16),
            pltpu.VMEM((WROWS, D), BF16),
            pltpu.VMEM((NSEQ, rows_out, D), BF16),
            pltpu.VMEM((BLK, D), BF16),
            pltpu.VMEM((rows_out, D), F32),
            dma((NSEQ,)),
            dma((NSEQ,)),
            dma((3, NSEQ)),
            dma((3, NSEQ)),
            dma((8,)),
            dma((9,)),
            dma((8,)),
            dma((8,)),
            dma((NSEQ,)),
            dma((NSEQ,)),
            dma((8,)),
        ],
        compiler_params=pltpu.CompilerParams(collective_id=1, has_side_effects=True),
        name="collect",
    )(o, dq, dk, dv, w, cot)


def local(queries, key_rows, values, adjacency, counts, out_weight, out_cotangent):
    cot = out_cotangent[0]
    qh, kh, vh, gh, w = spread(queries[0], key_rows[0], values[0], cot, out_weight)
    o, dq, dk, dv = attention(adjacency, counts, qh, kh, vh, gh)
    out, dq, dk, dv, wg = collect(o, dq, dk, dv, w, cot)
    return out[None], dq[None], dk[None], dv[None], wg


def solution(mesh):
    tokens = P("dp", "seq", None)
    in_specs = (tokens, tokens, tokens, P("dp", None, None), P("dp", None), P("dp", None), tokens)
    out_specs = (tokens,) * 4 + (P(("dp", "seq"), None),)
    return jax.shard_map(local, mesh=mesh, in_specs=in_specs, out_specs=out_specs, check_vma=False)
```

```python
import functools

import jax
import jax.numpy as jnp
from jax import lax
from jax.experimental import pallas as pl
from jax.experimental.pallas import tpu as pltpu
from jax.sharding import PartitionSpec as P

MESH = pl.DeviceIdType.MESH
HD = 128
BLK = 128
NBR = 8
NSEQ = 16
NDP = 8
NZ = 4
D = 2048
LEN = 2048
WROWS = D // NDP
SCALE = HD ** (-0.5)
F32 = jnp.float32
BF16 = jnp.bfloat16


def place():
    dp = lax.axis_index("dp")
    seq = lax.axis_index("seq")
    return dp, seq, dp // 2, dp % 2


def other_dp(z, c, dz, dc):
    return lax.rem(z + dz, NZ) * 2 + (lax.rem(c + dc, 2))


def remote(src, dst, send_sem, recv_sem, dp, seq):
    return pltpu.make_async_remote_copy(
        src_ref=src,
        dst_ref=dst,
        send_sem=send_sem,
        recv_sem=recv_sem,
        device_id=(dp, seq),
        device_id_type=MESH,
    )


def greet(partners):
    barrier = pltpu.get_barrier_semaphore()
    for dp, seq in partners:
        pl.semaphore_signal(barrier, inc=1, device_id=(dp, seq), device_id_type=MESH)
    pl.semaphore_wait(barrier, len(partners))


class DpGather:
    def __init__(self, own, slots, send_sem, recv_sem):
        self.dp, self.seq, self.z, self.c = place()
        self.own, self.slots, self.send_sem, self.recv_sem = own, slots, send_sem, recv_sem
        self.half = own.shape[0] // 2
        self.sends = []

    def dev(self, dz, dc):
        return other_dp(self.z, self.c, dz, dc)

    def send(self, src, dst, recv, dz, dc):
        copy = remote(
            src, dst, self.send_sem.at[len(self.sends)], self.recv_sem.at[recv], self.dev(dz, dc), self.seq
        )
        copy.start()
        self.sends.append(copy)

    def start(self):
        self.send(self.own, self.slots.at[6], 6, 1, 0)
        self.send(self.own, self.slots.at[2], 2, 3, 0)
        self.send(self.own, self.slots.at[1], 1, 0, 1)

    def await_slot(self, ref, recv):
        remote(ref, ref, self.send_sem.at[0], self.recv_sem.at[recv], self.dp, self.seq).wait_recv()

    def arrive(self, o):
        half = self.half
        if o == 4:
            self.await_slot(self.slots.at[4, pl.ds(0, half)], 4)
            self.await_slot(self.slots.at[4, pl.ds(half, half)], 8)
        else:
            self.await_slot(self.slots.at[o], o)
        if o == 2:
            self.send(self.slots.at[2, pl.ds(0, half)], self.slots.at[4, pl.ds(0, half)], 4, 3, 0)
        if o == 6:
            self.send(self.slots.at[6, pl.ds(half, half)], self.slots.at[4, pl.ds(half, half)], 8, 1, 0)
        if o in (2, 4, 6):
            self.send(self.slots.at[o], self.slots.at[o + 1], o + 1, 0, 1)

    def finish(self):
        for copy in self.sends:
            copy.wait_send()


GATHER_ORDER = (0, 1, 2, 6, 3, 7, 4, 5)


def spread_kernel(
    q_ref, k_ref, v_ref, cot_hbm, w_hbm,
    qh_ref, kh_ref, vh_ref, gh_ref, wfull_ref,
    cot, wbuf, gbuf,
    a2a_send, a2a_recv, g_send, g_recv, w_send, w_recv, loc_sem, own_sem, wout_sem,
):
    dp, seq, z, c = place()
    greet(
        [(dp, lax.rem(seq + r, NSEQ)) for r in range(1, NSEQ)]
        + [(other_dp(z, c, dz, dc), seq) for dz, dc in ((1, 0), (3, 0), (0, 1))]
    )
    load_cot = pltpu.make_async_copy(cot_hbm, cot, loc_sem.at[0])
    load_cot.start()
    load_w = pltpu.make_async_copy(w_hbm, wbuf.at[0], loc_sem.at[1])
    load_w.start()
    gather = DpGather(w_hbm, wbuf, w_send, w_recv)
    gather.start()
    here = pl.ds(pl.multiple_of(seq * BLK, BLK), BLK)
    pairs = ((q_ref, qh_ref), (k_ref, kh_ref), (v_ref, vh_ref))
    copies = []
    own_copies = []
    for n, (src, dst) in enumerate(pairs):
        for r in range(1, NSEQ):
            to = lax.rem(seq + r, NSEQ)
            copy = remote(
                src.at[:, pl.ds(pl.multiple_of(to * HD, HD), HD)],
                dst.at[here],
                a2a_send.at[n, r],
                a2a_recv.at[n, r],
                dp,
                to,
            )
            copy.start()
            copies.append(copy)
        copy = pltpu.make_async_copy(
            src.at[:, pl.ds(pl.multiple_of(seq * HD, HD), HD)], dst.at[here], own_sem.at[n]
        )
        copy.start()
        own_copies.append(copy)

    load_cot.wait()
    load_w.wait()
    wout = []

    def ship(o):
        owner = other_dp(z, c, o // 2, o % 2)
        for j in range(2):
            head = owner * 2 + j
            r = lax.rem(head - seq + NSEQ, NSEQ)
            src = gbuf.at[2 * o + j]

            @pl.when(r != 0)
            def _():
                remote(src, gh_ref.at[here], g_send.at[2 * o + j], g_recv.at[r], dp, head).start()

            @pl.when(r == 0)
            def _():
                pltpu.make_async_copy(src, gh_ref.at[here], g_send.at[2 * o + j]).start()

    last = None
    for o in GATHER_ORDER:
        if o:
            gather.arrive(o)
        owner = other_dp(z, c, o // 2, o % 2)
        copy = pltpu.make_async_copy(
            wbuf.at[o], wfull_ref.at[pl.ds(pl.multiple_of(owner * WROWS, WROWS), WROWS)], wout_sem.at[o]
        )
        copy.start()
        wout.append(copy)
        block = lax.dot_general(cot[...], wbuf[o], (((1,), (1,)), ((), ())), preferred_element_type=F32)
        for j in range(2):
            gbuf[2 * o + j] = block[:, j * HD : (j + 1) * HD].astype(BF16)
        if last is not None:
            ship(last)
        last = o
    ship(last)
    for copy in copies:
        copy.wait()
    for copy in own_copies + wout:
        copy.wait()
    gather.finish()
    for i in range(NSEQ):
        remote(gbuf.at[i], gbuf.at[i], g_send.at[i], g_recv.at[0], dp, seq).wait_send()
    for r in range(1, NSEQ):
        remote(gbuf.at[0], gh_ref.at[here], g_send.at[0], g_recv.at[r], dp, seq).wait_recv()


def spread(q, k, v, cot, w):
    head = jax.ShapeDtypeStruct((LEN, HD), BF16)
    any_spec = pl.BlockSpec(memory_space=pl.ANY)
    dma = pltpu.SemaphoreType.DMA
    return pl.pallas_call(
        spread_kernel,
        out_shape=(head, head, head, head, jax.ShapeDtypeStruct((D, D), BF16)),
        in_specs=[any_spec] * 5,
        out_specs=(any_spec,) * 5,
        scratch_shapes=[
            pltpu.VMEM((BLK, D), BF16),
            pltpu.VMEM((NDP, WROWS, D), BF16),
            pltpu.VMEM((NSEQ, BLK, HD), BF16),
            dma((3, NSEQ)),
            dma((3, NSEQ)),
            dma((NSEQ,)),
            dma((NSEQ,)),
            dma((8,)),
            dma((9,)),
            dma((2,)),
            dma((3,)),
            dma((NDP,)),
        ],
        compiler_params=pltpu.CompilerParams(collective_id=0, has_side_effects=True),
        name="spread",
    )(q, k, v, cot, w)


def attention_kernel(
    adj_ref, cnt_ref, q_ref, k_ref, v_ref, g_ref,
    o_ref, dq_ref, dk_ref, dv_ref,
    kt, vt, kg, vg, kgt, vgt, dk_acc, dv_acc,
):
    dk_acc[...] = jnp.zeros_like(dk_acc)
    dv_acc[...] = jnp.zeros_like(dv_acc)

    @pl.loop(0, LEN // BLK)
    def _(i):
        rows = pl.ds(pl.multiple_of(i * BLK, BLK), BLK)
        kt[i] = k_ref[rows, :].T
        vt[i] = v_ref[rows, :].T

    def run(i, slots):
        keys = slots * BLK
        rows = pl.ds(pl.multiple_of(i * BLK, BLK), BLK)
        q = q_ref[rows, :]
        g = g_ref[rows, :]
        count = cnt_ref[0, i]
        for j in range(slots):
            near = adj_ref[0, i, j]
            src = pl.ds(pl.multiple_of(near * BLK, BLK), BLK)
            dst = slice(j * BLK, (j + 1) * BLK)
            kg[dst, :] = k_ref[src, :]
            vg[dst, :] = v_ref[src, :]
            kgt[:, dst] = kt[near]
            vgt[:, dst] = vt[near]
        s = lax.dot_general(kg[:keys, :], q, (((1,), (1,)), ((), ())), preferred_element_type=F32) * SCALE
        live = lax.broadcasted_iota(jnp.int32, (keys, BLK), 0) < count * BLK
        s = jnp.where(live, s, -1e30)
        e = jnp.exp(s - jnp.max(s, axis=0, keepdims=True))
        p = e * (1.0 / jnp.sum(e, axis=0, keepdims=True))
        pb = p.astype(BF16)
        ot = jnp.dot(vgt[:, :keys], pb, preferred_element_type=F32)
        o_ref[rows, :] = ot.T.astype(BF16)
        dp = lax.dot_general(vg[:keys, :], g, (((1,), (1,)), ((), ())), preferred_element_type=F32)
        delta = jnp.sum(p * dp, axis=0, keepdims=True)
        ds = (p * (dp - delta) * SCALE).astype(BF16)
        dqt = jnp.dot(kgt[:, :keys], ds, preferred_element_type=F32)
        dq_ref[rows, :] = dqt.T.astype(BF16)
        dv = jnp.dot(pb, g, preferred_element_type=F32)
        dk = jnp.dot(ds, q, preferred_element_type=F32)
        for j in range(slots):
            near = adj_ref[0, i, j]
            dst = pl.ds(pl.multiple_of(near * BLK, BLK), BLK)
            part = slice(j * BLK, (j + 1) * BLK)
            dv_acc[dst, :] += dv[part, :]
            dk_acc[dst, :] += dk[part, :]

    @pl.loop(0, LEN // BLK)
    def _(i):
        count = cnt_ref[0, i]
        for slots in (2, 4, 6, 8):

            @pl.when((count > slots - 2) & (count <= slots))
            def _():
                run(i, slots)

    dk_ref[...] = dk_acc[...].astype(BF16)
    dv_ref[...] = dv_acc[...].astype(BF16)


def attention(adjacency, counts, q, k, v, g):
    head = jax.ShapeDtypeStruct((LEN, HD), BF16)
    vmem = pl.BlockSpec(memory_space=pltpu.VMEM)
    smem = pl.BlockSpec(memory_space=pltpu.SMEM)
    keys = NBR * BLK
    return pl.pallas_call(
        attention_kernel,
        out_shape=(head,) * 4,
        in_specs=[smem, smem] + [vmem] * 4,
        out_specs=(vmem,) * 4,
        scratch_shapes=[
            pltpu.VMEM((LEN // BLK, HD, BLK), BF16),
            pltpu.VMEM((LEN // BLK, HD, BLK), BF16),
            pltpu.VMEM((keys, HD), BF16),
            pltpu.VMEM((keys, HD), BF16),
            pltpu.VMEM((HD, keys), BF16),
            pltpu.VMEM((HD, keys), BF16),
            pltpu.VMEM((LEN, HD), F32),
            pltpu.VMEM((LEN, HD), F32),
        ],
        name="attention",
    )(adjacency, counts, q, k, v, g)


class Line:
    def __init__(self, src, dst, relay, sems, lo, n, x_first):
        self.dp, self.seq, _, _ = place()
        self.y, self.x = self.seq // 4, self.seq % 4
        self.src, self.dst, self.relay, self.sems = src, dst, relay, sems
        self.rows, self.x_first = pl.ds(lo, n), x_first

    def turn(self, r, along_x):
        if along_x:
            to = lax.rem(self.x + r, 4)
            return to, self.y * 4 + to
        to = lax.rem(self.y + r, 4)
        return to, to * 4 + self.x

    def put(self, r, src, dst, phase, to):
        if r:
            remote(src, dst, self.sems.at[3 * phase], self.sems.at[3 * phase + 1], self.dp, to).start()
        else:
            pltpu.make_async_copy(src, dst, self.sems.at[3 * phase + 2]).start()

    def start(self):
        for r in (1, 2, 3, 0):
            to, seq = self.turn(r, self.x_first)
            if self.x_first:
                at = pl.ds(pl.multiple_of(self.x * HD, HD), HD)
                for ty in range(4):
                    self.put(r, self.src.at[ty * 4 + to, self.rows], self.relay.at[ty, :, at], 0, seq)
            else:
                self.put(r, self.src.at[pl.ds(to * 4, 4), self.rows], self.relay.at[self.y], 0, seq)

    def block(self, sem):
        three = self.relay.at[pl.ds(0, 3)]
        return remote(three, three, self.sems.at[sem - 1 if sem % 3 else sem], self.sems.at[sem], self.dp, self.seq)

    def arrived(self, phase):
        one = self.relay.at[0]
        pltpu.make_async_copy(one, one, self.sems.at[3 * phase + 2]).wait()
        self.block(3 * phase + 1).wait_recv()

    def forward(self):
        self.arrived(0)
        for r in (1, 2, 3, 0):
            to, seq = self.turn(r, not self.x_first)
            if self.x_first:
                at = pl.ds(pl.multiple_of(self.y * 4 * HD, 4 * HD), 4 * HD)
                self.put(r, self.relay.at[to], self.dst.at[self.rows, at], 1, seq)
            else:
                for ys in range(4):
                    at = pl.ds(pl.multiple_of((ys * 4 + self.x) * HD, HD), HD)
                    self.put(r, self.relay.at[ys, to], self.dst.at[self.rows, at], 1, seq)

    def finish(self):
        self.arrived(1)

    def sent(self):
        for phase in range(2):
            self.block(3 * phase).wait_send()


class LineSum:
    def __init__(self, part, got, mid, last, sems, lo, n, x_first):
        self.dp, self.seq, _, _ = place()
        self.y, self.x = self.seq // 4, self.seq % 4
        self.part, self.got, self.mid, self.last, self.sems = part, got, mid, last, sems
        self.cols, self.x_first = pl.ds(lo, n), x_first

    turn = Line.turn

    def start(self):
        for r in (1, 2, 3):
            to, seq = self.turn(r, self.x_first)
            if self.x_first:
                for ty in range(4):
                    remote(
                        self.part.at[ty * 4 + to, :, self.cols], self.got.at[r - 1, ty],
                        self.sems.at[0], self.sems.at[1], self.dp, seq,
                    ).start()
            else:
                remote(
                    self.part.at[pl.ds(to * 4, 4), :, self.cols], self.got.at[r - 1],
                    self.sems.at[0], self.sems.at[1], self.dp, seq,
                ).start()

    def add(self):
        remote(self.got, self.got, self.sems.at[0], self.sems.at[1], self.dp, self.seq).wait_recv()
        for n in range(4):
            own = n * 4 + self.x if self.x_first else self.y * 4 + n
            total = self.part[own, :, self.cols].astype(F32)
            for r in range(3):
                total += self.got[r, n].astype(F32)
            self.mid[n] = total.astype(BF16)

    def forward(self):
        for r in (1, 2, 3):
            to, seq = self.turn(r, not self.x_first)
            remote(
                self.mid.at[to], self.last.at[r - 1], self.sems.at[2], self.sems.at[3], self.dp, seq
            ).start()

    def total(self):
        remote(self.last, self.last, self.sems.at[2], self.sems.at[3], self.dp, self.seq).wait_recv()
        total = self.mid[self.y if self.x_first else self.x].astype(F32)
        for r in range(3):
            total += self.last[r].astype(F32)
        return total

    def sent(self):
        remote(self.got, self.got, self.sems.at[0], self.sems.at[1], self.dp, self.seq).wait_send()
        remote(self.last, self.last, self.sems.at[2], self.sems.at[3], self.dp, self.seq).wait_send()


def line_partners(dp, seq):
    y, x = seq // 4, seq % 4
    return [(dp, y * 4 + lax.rem(x + r, 4)) for r in (1, 2, 3)] + [
        (dp, lax.rem(y + r, 4) * 4 + x) for r in (1, 2, 3)
    ]


def collect_kernel(
    o_hbm, dq_hbm, dk_hbm, dv_hbm, w_hbm, cot_hbm,
    out_ref, dq_ref, dk_ref, dv_ref, wg_ref,
    w, cg, cols, near, near_t, part, out_buf, wg_buf,
    o_relay_x, o_relay_y, q_relay, k_relay, v_relay_x, v_relay_y,
    got_x, got_y, mid_x, mid_y, last_x, last_y,
    line_sem, sum_sem, c_send, c_recv, n_send, n_recv, loc_sem,
):
    dp, seq, z, c = place()
    offsets = [(dz, dc) for dz in range(NZ) for dc in range(2) if dz or dc]
    greet(line_partners(dp, seq) + [(other_dp(z, c, dz, dc), seq) for dz, dc in offsets])
    half = BLK // 2
    o_x = Line(o_hbm, cols, o_relay_x, line_sem.at[0], 0, half, True)
    o_y = Line(o_hbm, cols, o_relay_y, line_sem.at[1], half, half, False)
    v_x = Line(dv_hbm, dv_ref, v_relay_x, line_sem.at[2], 0, half, True)
    v_y = Line(dv_hbm, dv_ref, v_relay_y, line_sem.at[3], half, half, False)
    q_x = Line(dq_hbm, dq_ref, q_relay, line_sem.at[4], 0, BLK, True)
    k_y = Line(dk_hbm, dk_ref, k_relay, line_sem.at[5], 0, BLK, False)
    gather = DpGather(cot_hbm, cg, c_send, c_recv)
    o_x.start()
    o_y.start()
    gather.start()
    v_x.start()
    v_y.start()
    load_cot = pltpu.make_async_copy(cot_hbm, cg.at[0], loc_sem.at[1])
    load_cot.start()
    load_w = pltpu.make_async_copy(w_hbm, w, loc_sem.at[2])
    load_w.start()
    o_x.forward()
    o_y.forward()
    q_x.start()
    k_y.start()
    v_x.forward()
    v_y.forward()
    o_x.finish()
    o_y.finish()

    near_copies = []
    for n, (dz, dc) in enumerate(offsets):
        to = other_dp(z, c, dz, dc)
        o = ((NZ - dz) % NZ) * 2 + dc
        copy = remote(
            cols.at[:, pl.ds(pl.multiple_of(to * WROWS, WROWS), WROWS)],
            near.at[pl.ds(o * BLK, BLK)],
            n_send.at[n],
            n_recv.at[o],
            to,
            seq,
        )
        copy.start()
        near_copies.append(copy)
    near[pl.ds(0, BLK), :] = cols[:, pl.ds(pl.multiple_of(dp * WROWS, WROWS), WROWS)]
    gather.arrive(1)
    gather.arrive(2)
    gather.arrive(6)
    q_x.forward()
    k_y.forward()

    load_w.wait()

    @pl.loop(0, D // 256)
    def _(n):
        at = pl.ds(pl.multiple_of(n * 256, 256), 256)
        out_buf[:, at] = jnp.dot(cols[...], w[:, at], preferred_element_type=F32).astype(BF16)

    store_out = pltpu.make_async_copy(out_buf, out_ref, loc_sem.at[6])
    store_out.start()

    load_cot.wait()
    for o in (3, 7, 4, 5):
        gather.arrive(o)
    for copy in near_copies:
        copy.wait_recv()
    near_t[...] = near[...].T
    rows_out = D // (NDP * NSEQ)

    def multiply(lo, hi):
        @pl.loop(lo // 256, hi // 256)
        def _(n):
            at = pl.ds(pl.multiple_of(n * 256, 256), 256)
            total = jnp.zeros((WROWS, 256), F32)
            for o in range(NDP):
                total += jnp.dot(near_t[:, o * BLK : (o + 1) * BLK], cg[o, :, at], preferred_element_type=F32)
            part[:, :, at] = total.astype(BF16).reshape(NSEQ, rows_out, 256)

    w_x = LineSum(part, got_x, mid_x, last_x, sum_sem.at[0], 0, D // 2, True)
    w_y = LineSum(part, got_y, mid_y, last_y, sum_sem.at[1], D // 2, D // 2, False)
    multiply(0, D // 2)
    w_x.start()
    multiply(D // 2, D)
    w_y.start()
    w_x.add()
    w_x.forward()
    w_y.add()
    w_y.forward()
    wg_buf[:, : D // 2] = w_x.total()
    wg_buf[:, D // 2 :] = w_y.total()
    store_wg = pltpu.make_async_copy(wg_buf, wg_ref, loc_sem.at[7])
    store_wg.start()

    for line in (v_x, v_y, q_x, k_y):
        line.finish()
    for line in (o_x, o_y, v_x, v_y, q_x, k_y, w_x, w_y):
        line.sent()
    for copy in near_copies:
        copy.wait_send()
    gather.finish()
    store_out.wait()
    store_wg.wait()


def collect(o, dq, dk, dv, w, cot):
    tokens = jax.ShapeDtypeStruct((BLK, D), BF16)
    any_spec = pl.BlockSpec(memory_space=pl.ANY)
    dma = pltpu.SemaphoreType.DMA
    rows_out = D // (NDP * NSEQ)
    half = BLK // 2
    blocks = (NSEQ, BLK, HD)
    return pl.pallas_call(
        collect_kernel,
        out_shape=(tokens,) * 4 + (jax.ShapeDtypeStruct((rows_out, D), F32),),
        in_specs=[any_spec] * 6,
        out_specs=(any_spec,) * 5,
        scratch_shapes=[
            pltpu.VMEM((D, D), BF16),
            pltpu.VMEM((NDP, BLK, D), BF16),
            pltpu.VMEM((BLK, D), BF16),
            pltpu.VMEM((NDP * BLK, WROWS), BF16),
            pltpu.VMEM((WROWS, NDP * BLK), BF16),
            pltpu.VMEM((NSEQ, rows_out, D), BF16),
            pltpu.VMEM((BLK, D), BF16),
            pltpu.VMEM((rows_out, D), F32),
            pltpu.VMEM((4, half, 4 * HD), BF16),
            pltpu.VMEM((4, 4, half, HD), BF16),
            pltpu.VMEM((4, BLK, 4 * HD), BF16),
            pltpu.VMEM((4, 4, BLK, HD), BF16),
            pltpu.VMEM((4, half, 4 * HD), BF16),
            pltpu.VMEM((4, 4, half, HD), BF16),
            pltpu.VMEM((3, 4, rows_out, D // 2), BF16),
            pltpu.VMEM((3, 4, rows_out, D // 2), BF16),
            pltpu.VMEM((4, rows_out, D // 2), BF16),
            pltpu.VMEM((4, rows_out, D // 2), BF16),
            pltpu.VMEM((3, rows_out, D // 2), BF16),
            pltpu.VMEM((3, rows_out, D // 2), BF16),
            dma((6, 6)),
            dma((2, 4)),
            dma((8,)),
            dma((9,)),
            dma((8,)),
            dma((8,)),
            dma((8,)),
        ],
        compiler_params=pltpu.CompilerParams(collective_id=1, has_side_effects=True),
        name="collect",
    )(o.reshape(blocks), dq.reshape(blocks), dk.reshape(blocks), dv.reshape(blocks), w, cot)


def deliver_kernel(*refs):
    count = (len(refs) - 1) // 3
    ins, outs, bufs, sem = refs[:count], refs[count : 2 * count], refs[2 * count : 3 * count], refs[-1]
    reads = [pltpu.make_async_copy(ins[n], bufs[n], sem.at[n]) for n in range(count)]
    writes = [pltpu.make_async_copy(bufs[n], outs[n], sem.at[count + n]) for n in range(count)]
    for copy in reads:
        copy.start()
    for n in range(count):
        reads[n].wait()
        writes[n].start()
    for copy in writes:
        copy.wait()


def deliver(*arrays):
    any_spec = pl.BlockSpec(memory_space=pl.ANY)
    return pl.pallas_call(
        deliver_kernel,
        out_shape=tuple(jax.ShapeDtypeStruct(a.shape, a.dtype) for a in arrays),
        in_specs=[any_spec] * len(arrays),
        out_specs=(any_spec,) * len(arrays),
        scratch_shapes=[pltpu.VMEM(a.shape, a.dtype) for a in arrays]
        + [pltpu.SemaphoreType.DMA((2 * len(arrays),))],
        name="deliver",
    )(*arrays)


def local(queries, key_rows, values, adjacency, counts, out_weight, out_cotangent):
    cot = out_cotangent[0]
    qh, kh, vh, gh, w = spread(queries[0], key_rows[0], values[0], cot, out_weight)
    o, dq, dk, dv = attention(adjacency, counts, qh, kh, vh, gh)
    out, dq, dk, dv, wg = deliver(*collect(o, dq, dk, dv, w, cot))
    return out[None], dq[None], dk[None], dv[None], wg


def solution(mesh):
    tokens = P("dp", "seq", None)
    in_specs = (tokens, tokens, tokens, P("dp", None, None), P("dp", None), P("dp", None), tokens)
    out_specs = (tokens,) * 4 + (P(("dp", "seq"), None),)
    return jax.shard_map(local, mesh=mesh, in_specs=in_specs, out_specs=out_specs, check_vma=False)
```
